128 devices in a mesh: req: 32 (over z, y, x_hi), tensor: 4 (over x_lo, core).
Axes of the slice: x: 4 (x_hi: 2, x_lo: 2; x = x_hi * 2 + x_lo), y: 4, z: 4, core: 2. Of those that a mesh axis runs over, the one named last changes fastest.
Arguments:
- span_in: bfloat16 [64, 512, 2048], P('req'), may hold values from -6 to 6
- w_qkv: bfloat16 [3, 2048, 2048], P(None, None, 'tensor'), may hold values from -1 to 1
- qk_gain: bfloat16 [2, 2048], P(None, 'tensor'), may hold values from 0.099609375 to 1.8984375
- w_out: bfloat16 [2048, 2048], P('tensor'), may hold values from -1 to 1
- post_gain: bfloat16 [2048], P('tensor'), may hold values from 0.099609375 to 1.8984375
- kv_pool: bfloat16 [4, 2048, 16, 2048], P(None, 'req', None, 'tensor'), may hold values from -66 to 66
- block_table: int32 [64, 32], replicated, may hold values from 0 to 63, as said below
- request_order: int32 [64], replicated, may hold values from 0 to 63, each once
- lengths: int32 [64], replicated, may hold values from 1 to 512, as said below
Outputs:
- span_out: bfloat16 [64, 512, 2048], P('req', None, 'tensor')
- relaid_cache: bfloat16 [4, 64, 512, 2048], P(None, 'req', None, 'tensor')
The draws below stay inside these ranges and needn't reach their ends.
Inputs may be any that keep to these rules, and one draw needn't show every extreme that they name: `block_table`: entry (r, j) is the slot, among the 64 slots of the req index j modulo the number of req devices, that holds block j of request r; each slot of each req index is named once. `lengths`: some request has exactly 512 cached tokens.
All inputs are finite; a program needn't handle non-finite values.
Results may differ from the reference program's by a relative error of at most 0.0095.
Values may be sent and summed in bfloat16 or wider, within the bound.
A program may use at most 192 MiB of HBM per device.

```python
import jax
import jax.numpy as jnp
from jax import lax

D = 2048
HEADS = 16
HD = 128
LAY = 2
CTX = 512
BLK = 16
SPAN = 512
REQS = 64
BPD = 1
SLOTS = 64
N_REQ = 32
N_TENSOR = 4


def normal_clipped(key, shape_all):
    return jnp.clip(jax.random.normal(key, shape_all, jnp.float32), -6.0, 6.0)


def draw_w_qkv(key, part):
    shape_all = (3, D, D)
    values = normal_clipped(key, shape_all)
    return (values * D ** (-0.5)).astype(jnp.bfloat16)


def draw_w_out(key, part):
    shape_all = (D, D)
    values = normal_clipped(key, shape_all)
    return (values * D ** (-0.5)).astype(jnp.bfloat16)


def draw_block_table(key, part):
    subkeys = jax.random.split(key, N_REQ)

    def one_device(subkey):
        return jax.random.permutation(subkey, SLOTS)
    permuted = jax.vmap(one_device)(subkeys)
    shaped = permuted.reshape(N_REQ, REQS, BPD)
    return jnp.transpose(shaped, (1, 2, 0)).reshape(REQS, BPD * N_REQ).astype(jnp.int32)


def draw_lengths(key, part):
    first_key, second_key = jax.random.split(key)
    drawn_lengths = jax.random.randint(first_key, (REQS,), 1, CTX + 1)
    longest = jax.random.randint(second_key, (), 0, REQS)
    return jnp.where(jnp.arange(REQS) == longest, CTX, drawn_lengths).astype(jnp.int32)


def draw_kv_pool(key, part):
    shape_all = (2 * LAY, N_REQ * SLOTS, BLK, D)
    base_key = jax.random.fold_in(key, 0)
    values = normal_clipped(base_key, shape_all)
    return values.astype(jnp.bfloat16)


def level_of(key, dims, pieces, least, top_value):
    level, own = 1.0, jax.random.fold_in(key, 6)
    for axis_at, shards_of in pieces:
        heights = jnp.exp(jax.random.uniform(jax.random.fold_in(own, axis_at), (shards_of,), jnp.float32, least / len(pieces), top_value / len(pieces)))
        level = level * jnp.repeat(heights, dims[axis_at] // shards_of).reshape([-1 if axis == axis_at else 1 for axis in range(len(dims))])
    return level


def bell_draw(key, dims, spread, limit, cuts=(), kind=jnp.bfloat16):
    values = spread * jax.random.normal(key, dims, jnp.float32)
    if cuts:
        values = values * level_of(key, dims, cuts, -0.22, 0.18)
    return jnp.clip(values, -limit, limit).astype(kind)


def setup_inputs(seed: int = 0) -> dict:
    splits = jax.random.split(jax.random.key(seed), 10)
    span_in = bell_draw(splits[0], (REQS, SPAN, D), 1.0, 6.0, ((0, 32),))
    w_qkv = draw_w_qkv(jax.random.fold_in(splits[9], 71), 0)
    qk_gain = jnp.clip(1.0 + 0.18 * jax.random.normal(splits[2], (2, D), jnp.float32), 0.099609375, 1.8984375).astype(jnp.bfloat16)
    w_out = draw_w_out(jax.random.fold_in(splits[9], 71), 0)
    post_gain = jnp.clip(1.0 + 0.18 * jax.random.normal(splits[4], (D,), jnp.float32), 0.099609375, 1.8984375).astype(jnp.bfloat16)
    kv_pool = draw_kv_pool(jax.random.fold_in(splits[9], 71), 0)
    block_table = draw_block_table(jax.random.fold_in(splits[9], 71), 0)
    request_order = jax.random.permutation(splits[7], REQS).astype(jnp.int32)
    lengths = draw_lengths(jax.random.fold_in(splits[9], 71), 0)
    return dict(span_in=span_in, w_qkv=w_qkv, qk_gain=qk_gain, w_out=w_out, post_gain=post_gain, kv_pool=kv_pool, block_table=block_table, request_order=request_order, lengths=lengths)


norm_eps = 1e-06
rope_base = 500000.0

def rotate(values, positions):
    half_dim = values.shape[-1] // 2
    frequency = rope_base ** (-jnp.arange(half_dim, dtype=jnp.float32) * (2.0 / values.shape[-1]))
    angles = positions[:, None] * frequency[None, :]
    cosine = jnp.cos(angles)[:, None, :]
    sine_part = jnp.sin(angles)[:, None, :]
    first_half = values[..., :half_dim]
    second_half = values[..., half_dim:]
    return jnp.concatenate([first_half * cosine - second_half * sine_part, second_half * cosine + first_half * sine_part], axis=-1)

def reference(span_in, w_qkv, qk_gain, w_out, post_gain, kv_pool, block_table, request_order, lengths):
    token_ids = jnp.arange(CTX, dtype=jnp.int32)
    block_ids = token_ids // BLK
    offsets = token_ids % BLK
    slot_ids = jnp.take(block_table, request_order, axis=0)[:, block_ids]
    global_slots = ((block_ids % N_REQ)[None, :] * SLOTS + slot_ids).astype(jnp.int32)
    relaid_cache = kv_pool[:, global_slots, offsets[None, :], :]
    ordered_lengths = jnp.take(lengths, request_order)
    part_width = D // N_TENSOR

    def one_request(inputs):
        tokens, cached_len, cache_keys, cache_values = inputs
        queries = jnp.dot(tokens, w_qkv[0], preferred_element_type=jnp.float32)
        keys_new = jnp.dot(tokens, w_qkv[1], preferred_element_type=jnp.float32)
        values_new = jnp.dot(tokens, w_qkv[2], preferred_element_type=jnp.float32).astype(jnp.bfloat16)
        queries = queries * lax.rsqrt(lax.optimization_barrier(jnp.mean(queries * queries, axis=-1, keepdims=True)) + norm_eps) * qk_gain[0].astype(jnp.float32)
        keys_new = keys_new * lax.rsqrt(lax.optimization_barrier(jnp.mean(keys_new * keys_new, axis=-1, keepdims=True)) + norm_eps) * qk_gain[1].astype(jnp.float32)
        positions = cached_len.astype(jnp.float32) + jnp.arange(SPAN, dtype=jnp.float32)
        query_rot = rotate(queries.reshape(SPAN, HEADS, HD), positions).astype(jnp.bfloat16)
        key_rot = rotate(keys_new.reshape(SPAN, HEADS, HD), positions).astype(jnp.bfloat16)
        all_keys = jnp.concatenate([cache_keys.reshape(CTX, HEADS, HD), key_rot], axis=0)
        all_values = jnp.concatenate([cache_values.reshape(CTX, HEADS, HD), values_new.reshape(SPAN, HEADS, HD)], axis=0)
        scores = jnp.einsum('qhd,khd->hqk', query_rot.astype(jnp.float32), all_keys.astype(jnp.float32)) * HD ** (-0.5)
        cache_live = jnp.arange(CTX, dtype=jnp.int32) < cached_len
        causal = jnp.arange(SPAN)[None, :] <= jnp.arange(SPAN)[:, None]
        live_mask = jnp.concatenate([jnp.broadcast_to(cache_live[None, :], (SPAN, CTX)), causal], axis=1)
        scores = jnp.where(live_mask[None], scores, -1e+30)
        maxima = lax.optimization_barrier(jnp.max(scores, axis=-1, keepdims=True))
        exponent = jnp.exp(scores - maxima)
        weights = (exponent / lax.optimization_barrier(jnp.sum(exponent, axis=-1, keepdims=True))).astype(jnp.bfloat16)
        attended = jnp.einsum('hqk,khd->qhd', weights.astype(jnp.float32), all_values.astype(jnp.float32))
        attended = attended.astype(jnp.bfloat16).reshape(SPAN, D)
        total_sum = jnp.zeros((SPAN, D), jnp.float32)
        for group_no in range(N_TENSOR):
            low = group_no * part_width
            partial_value = jnp.dot(attended[:, low:low + part_width], w_out[low:low + part_width], preferred_element_type=jnp.float32)
            rounded = lax.optimization_barrier(partial_value.astype(jnp.bfloat16))
            total_sum = total_sum + rounded.astype(jnp.float32)
        normed = total_sum * lax.rsqrt(lax.optimization_barrier(jnp.mean(total_sum * total_sum, axis=-1, keepdims=True)) + norm_eps)
        return (tokens.astype(jnp.float32) + normed * post_gain.astype(jnp.float32)).astype(jnp.bfloat16)
    span_out = lax.map(one_request, (span_in, ordered_lengths, relaid_cache[0], relaid_cache[1]))
    return (span_out, relaid_cache)
```

```python
import functools
import math

import jax
import jax.numpy as jnp
from jax import lax
from jax.experimental import pallas as pl
from jax.experimental.pallas import tpu as pltpu
from jax.sharding import PartitionSpec as P

MESH = pl.DeviceIdType.MESH
HD = 128
HALF = HD // 2
NORM_EPS = 1e-06
ROPE_BASE = 500000.0
GRID = (4, 4, 2)
NEG = -1e30


def far_first():
    steps = [
        (dz, dy, dx)
        for dz in range(GRID[0])
        for dy in range(GRID[1])
        for dx in range(GRID[2])
    ][1:]

    def hops(step):
        dz, dy, dx = step
        return min(dz, GRID[0] - dz) + min(dy, GRID[1] - dy) + 2 * dx

    return sorted(steps, key=lambda step: -hops(step))


def lane_fold(values):
    total = values[:, :HD]
    for low in range(HD, values.shape[1], HD):
        total = total + values[:, low : low + HD]
    return total


def rows_to_lanes(values):
    return jnp.sum(jnp.transpose(values), axis=0, keepdims=True)


def lanes_to_rows(row):
    return jnp.transpose(jnp.broadcast_to(row, (HD, HD)))


def kernel(
    table_ref,
    order_ref,
    length_ref,
    gain_ref,
    post_ref,
    x_hbm,
    wqkv_hbm,
    wout_hbm,
    pool_hbm,
    out_hbm,
    relaid_hbm,
    pool_a,
    pool_b,
    send_a,
    send_b,
    cache_v,
    x_v,
    w_v,
    wo_v,
    wp_v,
    qk_f,
    qk_b,
    v_b,
    fold_v,
    cos_v,
    sin_v,
    stat_s,
    stat_r,
    att_v,
    attp_v,
    part_s,
    part_r,
    tot_v,
    fin_s,
    fin_r,
    res_v,
    load_sem,
    store_sem,
    a2a_s,
    a2a_r,
    wp_ss,
    wp_rs,
    stat_ss,
    stat_rs,
    att_ss,
    att_rs,
    part_ss,
    part_rs,
    fin_ss,
    fin_rs,
):
    me = lax.axis_index("req")
    t = lax.axis_index("tensor")
    n_req = lax.axis_size("req")
    chip, core = t // 2, lax.rem(t, 2)
    t1 = chip * 2 + 1 - core
    t2 = (1 - chip) * 2 + core
    t3 = (1 - chip) * 2 + 1 - core
    peers = ((me, t1), (me, t2), (me, t3))
    x_at, y_at, z_at = lax.rem(me, 2), lax.rem(me // 2, 4), me // 8
    steps = far_first()

    def at_step(step):
        dz, dy, dx = step
        return (lax.rem(z_at + dz, 4) * 4 + lax.rem(y_at + dy, 4)) * 2 + lax.rem(
            x_at + dx, 2
        )

    targets = [at_step(step) for step in steps]
    span = x_hbm.shape[0] // 2
    width = x_hbm.shape[1]
    part = v_b.shape[1]
    heads = part // HD
    ctx = cache_v.shape[2]
    blk = pool_hbm.shape[2]
    n_pos = pool_hbm.shape[1]
    half = span // 2

    pool_in = [
        pltpu.make_async_copy(
            pool_hbm.at[pl.ds(2 * g, 2)], (pool_a, pool_b)[g], load_sem.at[g]
        )
        for g in range(2)
    ]
    x_in = [
        pltpu.make_async_copy(
            x_hbm.at[pl.ds(k * span, span)],
            x_v.at[pl.ds(k * span, span)],
            load_sem.at[2 + k],
        )
        for k in range(2)
    ]
    w_in = [
        pltpu.make_async_copy(wqkv_hbm.at[m], w_v.at[m], load_sem.at[4 + m])
        for m in range(3)
    ]
    wo_in = pltpu.make_async_copy(wout_hbm, wo_v, load_sem.at[7])
    barrier = pltpu.get_barrier_semaphore()
    for copy in pool_in:
        copy.start()
    for d in targets:
        pl.semaphore_signal(barrier, inc=1, device_id=(d, t), device_id_type=MESH)
    for peer in peers:
        pl.semaphore_signal(barrier, inc=1, device_id=peer, device_id_type=MESH)
    for copy in (x_in[0], w_in[0], w_in[1], x_in[1], w_in[2], wo_in):
        copy.start()

    sends = (send_a, send_b)

    def gather(g):
        pool_v, send_v = (pool_a, pool_b)[g], sends[g]

        def body(p, carry):
            slot = table_ref[order_ref[p], me]
            for plane in range(2):
                send_v[p // 2, plane, lax.rem(p, 2)] = pool_v[plane, slot]
            return carry

        lax.fori_loop(0, n_pos, body, 0, unroll=4)
        own = pl.ds(pl.multiple_of(me * blk, blk), blk)
        for plane in range(2):
            for k in range(2):
                cache_v[2 * g + plane, k, own, :] = send_v[me, plane, k]

    def handover(g):
        own = pl.ds(pl.multiple_of(me * blk, blk), blk)
        return [
            pltpu.make_async_remote_copy(
                sends[g].at[d],
                cache_v.at[pl.ds(2 * g, 2), :, own, :],
                a2a_s.at[g, i],
                a2a_r.at[g, i],
                device_id=(d, t),
                device_id_type=MESH,
            )
            for i, d in enumerate(targets)
        ]

    pool_in[0].wait()
    gather(0)
    pl.semaphore_wait(barrier, len(targets) + len(peers))
    moves = [handover(0), handover(1)]
    for copy in moves[0]:
        copy.start()
    pool_in[1].wait()
    gather(1)

    x_in[0].wait()
    x_in[1].wait()
    w_in[0].wait()
    w_in[1].wait()
    n_half = part // 2

    def qk_tile(i, carry):
        m, k, h = i // 4, lax.rem(i // 2, 2), lax.rem(i, 2)
        rows = pl.ds(pl.multiple_of(k * span, span), span)
        cols = pl.ds(pl.multiple_of(h * n_half, n_half), n_half)
        tile = jnp.dot(
            x_v[rows, :], w_v[m, :, cols], preferred_element_type=jnp.float32
        )
        qk_f[m, rows, cols] = tile
        fold = lane_fold(tile * tile)

        @pl.when(h == 0)
        def _():
            fold_v[m, rows, :] = fold

        @pl.when(h == 1)
        def _():
            fold_v[m, rows, :] = fold_v[m, rows, :] + fold

        return carry

    lax.fori_loop(0, 8, qk_tile, 0)
    groups = 2 * span // HD
    for m in range(2):
        for b in range(groups):
            stat_s[pl.ds(m * groups + b, 1), :] = rows_to_lanes(
                fold_v[m, pl.ds(b * HD, HD), :]
            )

    wo_in.wait()
    wp_moves = [
        pltpu.make_async_remote_copy(
            wo_v.at[:, pl.ds(pl.multiple_of(col * part, part), part)],
            wp_v.at[j],
            wp_ss.at[j],
            wp_rs.at[j],
            device_id=(me, t1),
            device_id_type=MESH,
        )
        for j, col in enumerate((t1, t3))
    ]
    for copy in wp_moves:
        copy.start()
    w_in[2].wait()

    def v_tile(i, carry):
        k, h = i // 2, lax.rem(i, 2)
        rows = pl.ds(pl.multiple_of(k * span, span), span)
        cols = pl.ds(pl.multiple_of(h * n_half, n_half), n_half)
        v_b[rows, cols] = jnp.dot(
            x_v[rows, :], w_v[2, :, cols], preferred_element_type=jnp.float32
        ).astype(jnp.bfloat16)
        return carry

    lax.fori_loop(0, 4, v_tile, 0)
    stat_moves = [
        pltpu.make_async_remote_copy(
            stat_s,
            stat_r.at[j],
            stat_ss.at[j],
            stat_rs.at[j],
            device_id=peer,
            device_id_type=MESH,
        )
        for j, peer in enumerate(peers)
    ]
    for copy in stat_moves:
        copy.start()
    for copy in moves[1]:
        copy.start()

    lens = [length_ref[order_ref[2 * me + k]] for k in range(2)]
    lane = lax.broadcasted_iota(jnp.int32, (1, HD), 1)
    pair = jnp.where(lane < HALF, lane, lane - HALF).astype(jnp.float32)
    frequency = jnp.exp(pair * (-2.0 / HD * math.log(ROPE_BASE)))
    for k in range(2):

        def angle_tile(b, carry, k=k):
            token = lax.broadcasted_iota(jnp.int32, (HD, 1), 0) + b * HD + lens[k]
            angle = token.astype(jnp.float32) * frequency
            rows = pl.ds(pl.multiple_of(k * span + b * HD, HD), HD)
            cos_v[rows, :] = jnp.cos(angle)
            sine = jnp.sin(angle)
            sin_v[rows, :] = jnp.where(lane < HALF, -sine, sine)
            return carry

        lax.fori_loop(0, span // HD, angle_tile, 0)

    for copy in stat_moves:
        copy.wait_recv()
    square = stat_s[...] + stat_r[0] + stat_r[1] + stat_r[2]
    scale = lax.rsqrt(square / width + NORM_EPS)
    for m in range(2):
        for b in range(groups):
            fold_v[m, pl.ds(b * HD, HD), :] = lanes_to_rows(
                scale[m * groups + b : m * groups + b + 1, :]
            )

    def rope_tile(b, carry):
        rows = pl.ds(pl.multiple_of(b * HD, HD), HD)
        cosine, sine = cos_v[rows, :], sin_v[rows, :]
        for m in range(2):
            by_row = fold_v[m, rows, :]
            for h in range(heads):
                cols = pl.ds(h * HD, HD)
                gain = gain_ref[m : m + 1, h * HD : (h + 1) * HD].astype(jnp.float32)
                value = qk_f[m, rows, cols] * by_row * gain
                turned = value * cosine + pltpu.roll(value, HALF, 1) * sine
                qk_b[m, rows, cols] = turned.astype(jnp.bfloat16)
        return carry

    lax.fori_loop(0, groups, rope_tile, 0)

    for copy in moves[0]:
        copy.wait_recv()
    relaid_out = [
        pltpu.make_async_copy(
            cache_v.at[pl.ds(2 * g, 2)], relaid_hbm.at[pl.ds(2 * g, 2)], store_sem.at[g]
        )
        for g in range(2)
    ]
    relaid_out[0].start()

    token_at = lax.broadcasted_iota(jnp.int32, (1, ctx), 1)
    to_base2 = HD**-0.5 * math.log2(math.e)
    causal = lax.broadcasted_iota(jnp.int32, (half, half), 1) <= (
        lax.broadcasted_iota(jnp.int32, (half, half), 0)
    )
    over_rows = (((1,), (1,)), ((), ()))

    def attend(i):
        k, q_at = i // 2, i % 2
        bias = jnp.where(token_at < lens[k], 0.0, NEG)
        seen = half * (q_at + 1)
        new_rows = pl.ds(k * span, seen)

        def head(h, carry):
            cols = pl.ds(pl.multiple_of(h * HD, HD), HD)
            query = qk_b[0, pl.ds(k * span + q_at * half, half), cols]
            old = (
                lax.dot_general(
                    query,
                    cache_v[0, k, :, cols],
                    over_rows,
                    preferred_element_type=jnp.float32,
                )
                + bias
            )
            new = lax.dot_general(
                query,
                qk_b[1, new_rows, cols],
                over_rows,
                preferred_element_type=jnp.float32,
            )
            last = jnp.where(causal, new[:, seen - half :], NEG)
            pieces = [old] + ([new[:, : seen - half]] if q_at else []) + [last]
            top = functools.reduce(
                jnp.maximum, [jnp.max(s, axis=1, keepdims=True) for s in pieces]
            )
            grown = [jnp.exp2((s - top) * to_base2) for s in pieces]
            norm = sum(jnp.sum(e, axis=1, keepdims=True) for e in grown)
            value = jnp.dot(
                grown[0].astype(jnp.bfloat16),
                cache_v[1, k, :, cols],
                preferred_element_type=jnp.float32,
            )
            for j, e in enumerate(grown[1:]):
                value = value + jnp.dot(
                    e.astype(jnp.bfloat16),
                    v_b[pl.ds(k * span + j * half, half), cols],
                    preferred_element_type=jnp.float32,
                )
            att_v[pl.ds(i * half, half), cols] = (value * (1.0 / norm)).astype(
                jnp.bfloat16
            )
            return carry

        lax.fori_loop(0, heads, head, 0)

    att_moves = [
        pltpu.make_async_remote_copy(
            att_v.at[pl.ds(i * half, half)],
            attp_v.at[pl.ds(i * half, half)],
            att_ss.at[i],
            att_rs.at[i],
            device_id=(me, t1),
            device_id_type=MESH,
        )
        for i in range(4)
    ]
    part_moves = [
        pltpu.make_async_remote_copy(
            part_s.at[pl.ds(i * half, half)],
            part_r.at[pl.ds(i * half, half)],
            part_ss.at[i],
            part_rs.at[i],
            device_id=(me, t2),
            device_id_type=MESH,
        )
        for i in range(4)
    ]

    def project(i):
        rows = pl.ds(i * half, half)

        def columns(j, col):
            cols = pl.ds(pl.multiple_of(col * part, part), part)
            return jnp.dot(
                att_v[rows, :], wo_v[:, cols], preferred_element_type=jnp.float32
            ) + jnp.dot(attp_v[rows, :], wp_v[j], preferred_element_type=jnp.float32)

        part_s[rows, :] = columns(1, t2).astype(jnp.bfloat16)
        tot_v[rows, :] = columns(0, t)

    for i in range(4):
        attend(i)
        if i:
            att_moves[i - 1].wait_recv()
            project(i - 1)
            part_moves[i - 1].start()
        att_moves[i].start()
        if i == 0:
            for copy in wp_moves:
                copy.wait_recv()
    att_moves[3].wait_recv()
    project(3)
    part_moves[3].start()

    for copy in moves[1]:
        copy.wait_recv()
    relaid_out[1].start()

    fin_moves = [
        [
            pltpu.make_async_remote_copy(
                fin_s.at[i],
                fin_r.at[i, j],
                fin_ss.at[i, j],
                fin_rs.at[i, j],
                device_id=peer,
                device_id_type=MESH,
            )
            for j, peer in enumerate(peers)
        ]
        for i in range(4)
    ]
    res_out = [
        pltpu.make_async_copy(
            res_v.at[pl.ds(i * half, half)],
            out_hbm.at[pl.ds(i * half, half)],
            store_sem.at[2 + i],
        )
        for i in range(4)
    ]
    own_cols = pl.ds(pl.multiple_of(t * part, part), part)

    def finish(i):
        for copy in fin_moves[i]:
            copy.wait_recv()
        square = fin_s[i] + fin_r[i, 0] + fin_r[i, 1] + fin_r[i, 2]
        scale = lax.rsqrt(square / width + NORM_EPS)
        post = post_ref[...].astype(jnp.float32)
        for b in range(half // HD):
            rows = pl.ds(i * half + b * HD, HD)
            by_row = lanes_to_rows(scale[b : b + 1, :])
            by_row = jnp.concatenate([by_row] * heads, axis=1)
            normed = tot_v[rows, :] * by_row * post
            res_v[rows, :] = (x_v[rows, own_cols].astype(jnp.float32) + normed).astype(
                jnp.bfloat16
            )
        res_out[i].start()

    for i in range(4):
        part_moves[i].wait_recv()
        fin_s[i] = jnp.zeros_like(fin_s[i])
        for b in range(half // HD):
            rows = pl.ds(i * half + b * HD, HD)
            total = tot_v[rows, :] + part_r[rows, :].astype(jnp.float32)
            tot_v[rows, :] = total
            fin_s[i, b : b + 1, :] = rows_to_lanes(lane_fold(total * total))
        for copy in fin_moves[i]:
            copy.start()
        if i:
            finish(i - 1)
    finish(3)

    for g in range(2):
        for copy in moves[g]:
            copy.wait_send()
    for copy in wp_moves + stat_moves + att_moves + part_moves:
        copy.wait_send()
    for group in fin_moves:
        for copy in group:
            copy.wait_send()
    for copy in relaid_out + res_out:
        copy.wait()


def on_device(
    span_in, w_qkv, qk_gain, w_out, post_gain, kv_pool, block_table, request_order, lengths
):
    per_device, span, width = span_in.shape
    part = w_qkv.shape[2]
    planes, n_pos, blk, _ = kv_pool.shape
    rows = per_device * span
    n_req = lax.axis_size("req")
    ctx = block_table.shape[1] * blk
    bf16, f32 = jnp.bfloat16, jnp.float32
    vmem, dma = pltpu.VMEM, pltpu.SemaphoreType.DMA
    smem = pl.BlockSpec(memory_space=pltpu.SMEM)
    in_vmem = pl.BlockSpec(memory_space=pltpu.VMEM)
    stay = pl.BlockSpec(memory_space=pl.ANY)
    stat_rows = 2 * rows // HD
    out, relaid = pl.pallas_call(
        kernel,
        name="handover_layer",
        out_shape=(
            jax.ShapeDtypeStruct((rows, part), bf16),
            jax.ShapeDtypeStruct((planes, per_device, ctx, part), bf16),
        ),
        in_specs=[smem] * 3 + [in_vmem] * 2 + [stay] * 4,
        out_specs=(stay, stay),
        scratch_shapes=[
            vmem((2, n_pos, blk, part), bf16),
            vmem((2, n_pos, blk, part), bf16),
            vmem((n_req, 2, per_device, blk, part), bf16),
            vmem((n_req, 2, per_device, blk, part), bf16),
            vmem((planes, per_device, ctx, part), bf16),
            vmem((rows, width), bf16),
            vmem((3, width, part), bf16),
            vmem((part, width), bf16),
            vmem((2, part, part), bf16),
            vmem((2, rows, part), f32),
            vmem((2, rows, part), bf16),
            vmem((rows, part), bf16),
            vmem((2, rows, HD), f32),
            vmem((rows, HD), f32),
            vmem((rows, HD), f32),
            vmem((stat_rows, HD), f32),
            vmem((3, stat_rows, HD), f32),
            vmem((rows, part), bf16),
            vmem((rows, part), bf16),
            vmem((rows, part), bf16),
            vmem((rows, part), bf16),
            vmem((rows, part), f32),
            vmem((4, 8, HD), f32),
            vmem((4, 3, 8, HD), f32),
            vmem((rows, part), bf16),
            dma((8,)),
            dma((6,)),
            dma((2, n_req)),
            dma((2, n_req)),
            dma((2,)),
            dma((2,)),
            dma((3,)),
            dma((3,)),
            dma((4,)),
            dma((4,)),
            dma((4,)),
            dma((4,)),
            dma((4, 3)),
            dma((4, 3)),
        ],
        compiler_params=pltpu.CompilerParams(
            collective_id=0, has_side_effects=True, vmem_limit_bytes=62 << 20
        ),
    )(
        block_table,
        request_order,
        lengths,
        qk_gain,
        post_gain.reshape(1, part),
        span_in.reshape(rows, width),
        w_qkv,
        w_out,
        kv_pool,
    )
    return out.reshape(per_device, span, part), relaid


def solution(mesh):
    placed = (
        P("req", None, None),
        P(None, None, "tensor"),
        P(None, "tensor"),
        P("tensor", None),
        P("tensor"),
        P(None, "req", None, "tensor"),
        P(),
        P(),
        P(),
    )
    return jax.shard_map(
        on_device,
        mesh=mesh,
        in_specs=placed,
        out_specs=(P("req", None, "tensor"), P(None, "req", None, "tensor")),
        check_vma=False,
    )
```

```python
import functools
import math

import jax
import jax.numpy as jnp
from jax import lax
from jax.experimental import pallas as pl
from jax.experimental.pallas import tpu as pltpu
from jax.sharding import PartitionSpec as P

MESH = pl.DeviceIdType.MESH
HD = 128
HALF = HD // 2
NORM_EPS = 1e-06
ROPE_BASE = 500000.0
GRID = (4, 4, 2)
NEG = -1e30


def far_first():
    steps = [
        (dz, dy, dx)
        for dz in range(GRID[0])
        for dy in range(GRID[1])
        for dx in range(GRID[2])
    ][1:]

    def hops(step):
        dz, dy, dx = step
        return min(dz, GRID[0] - dz) + min(dy, GRID[1] - dy) + 2 * dx

    return sorted(steps, key=lambda step: -hops(step))


def lane_fold(values):
    total = values[:, :HD]
    for low in range(HD, values.shape[1], HD):
        total = total + values[:, low : low + HD]
    return total


def rows_to_lanes(values):
    return jnp.sum(jnp.transpose(values), axis=0, keepdims=True)


def lanes_to_rows(row):
    return jnp.transpose(jnp.broadcast_to(row, (HD, HD)))


def kernel(
    table_ref,
    order_ref,
    length_ref,
    gain_ref,
    post_ref,
    x_hbm,
    wqkv_hbm,
    wout_hbm,
    pool_hbm,
    res_v,
    cache_v,
    pool_a,
    pool_b,
    send_a,
    send_b,
    x_v,
    w_v,
    wo_v,
    wp_v,
    qk_f,
    qk_b,
    v_b,
    fold_v,
    cos_v,
    sin_v,
    stat_s,
    stat_r,
    att_v,
    attp_v,
    part_s,
    part_r,
    tot_v,
    fin_s,
    fin_r,
    load_sem,
    a2a_s,
    a2a_r,
    wp_ss,
    wp_rs,
    stat_ss,
    stat_rs,
    att_ss,
    att_rs,
    part_ss,
    part_rs,
    fin_ss,
    fin_rs,
):
    me = lax.axis_index("req")
    t = lax.axis_index("tensor")
    n_req = lax.axis_size("req")
    chip, core = t // 2, lax.rem(t, 2)
    t1 = chip * 2 + 1 - core
    t2 = (1 - chip) * 2 + core
    t3 = (1 - chip) * 2 + 1 - core
    peers = ((me, t1), (me, t2), (me, t3))
    x_at, y_at, z_at = lax.rem(me, 2), lax.rem(me // 2, 4), me // 8
    steps = far_first()

    def at_step(step):
        dz, dy, dx = step
        return (lax.rem(z_at + dz, 4) * 4 + lax.rem(y_at + dy, 4)) * 2 + lax.rem(
            x_at + dx, 2
        )

    targets = [at_step(step) for step in steps]
    span = x_hbm.shape[0] // 2
    width = x_hbm.shape[1]
    part = v_b.shape[1]
    heads = part // HD
    ctx = cache_v.shape[2]
    blk = pool_hbm.shape[2]
    n_pos = pool_hbm.shape[1]
    half = span // 2

    pool_in = [
        pltpu.make_async_copy(
            pool_hbm.at[pl.ds(2 * g, 2)], (pool_a, pool_b)[g], load_sem.at[g]
        )
        for g in range(2)
    ]
    x_in = [
        pltpu.make_async_copy(
            x_hbm.at[pl.ds(k * span, span)],
            x_v.at[pl.ds(k * span, span)],
            load_sem.at[2 + k],
        )
        for k in range(2)
    ]
    w_in = [
        pltpu.make_async_copy(wqkv_hbm.at[m], w_v.at[m], load_sem.at[4 + m])
        for m in range(3)
    ]
    wo_in = pltpu.make_async_copy(wout_hbm, wo_v, load_sem.at[7])
    barrier = pltpu.get_barrier_semaphore()
    for copy in pool_in:
        copy.start()
    for d in targets:
        pl.semaphore_signal(barrier, inc=1, device_id=(d, t), device_id_type=MESH)
    for peer in peers:
        pl.semaphore_signal(barrier, inc=1, device_id=peer, device_id_type=MESH)
    for copy in (x_in[0], w_in[0], w_in[1], x_in[1], w_in[2], wo_in):
        copy.start()

    sends = (send_a, send_b)

    def gather(g):
        pool_v, send_v = (pool_a, pool_b)[g], sends[g]

        def body(p, carry):
            slot = table_ref[me, order_ref[p]]
            for plane in range(2):
                send_v[p // 2, plane, lax.rem(p, 2)] = pool_v[plane, slot]
            return carry

        lax.fori_loop(0, n_pos, body, 0, unroll=4)
        own = pl.ds(pl.multiple_of(me * blk, blk), blk)
        for plane in range(2):
            for k in range(2):
                cache_v[2 * g + plane, k, own, :] = send_v[me, plane, k]

    def handover(g):
        own = pl.ds(pl.multiple_of(me * blk, blk), blk)
        return [
            pltpu.make_async_remote_copy(
                sends[g].at[d],
                cache_v.at[pl.ds(2 * g, 2), :, own, :],
                a2a_s.at[g, i],
                a2a_r.at[g, i],
                device_id=(d, t),
                device_id_type=MESH,
            )
            for i, d in enumerate(targets)
        ]

    pool_in[0].wait()
    gather(0)
    pl.semaphore_wait(barrier, len(targets) + len(peers))
    moves = [handover(0), handover(1)]
    for copy in moves[0]:
        copy.start()
    pool_in[1].wait()
    gather(1)

    x_in[0].wait()
    x_in[1].wait()
    w_in[0].wait()
    w_in[1].wait()
    n_half = part // 2

    def qk_tile(i, carry):
        m, k, h = i // 4, lax.rem(i // 2, 2), lax.rem(i, 2)
        rows = pl.ds(pl.multiple_of(k * span, span), span)
        cols = pl.ds(pl.multiple_of(h * n_half, n_half), n_half)
        tile = jnp.dot(
            x_v[rows, :], w_v[m, :, cols], preferred_element_type=jnp.float32
        )
        qk_f[m, rows, cols] = tile
        fold = lane_fold(tile * tile)

        @pl.when(h == 0)
        def _():
            fold_v[m, rows, :] = fold

        @pl.when(h == 1)
        def _():
            fold_v[m, rows, :] = fold_v[m, rows, :] + fold

        return carry

    lax.fori_loop(0, 8, qk_tile, 0)
    groups = 2 * span // HD
    for m in range(2):
        for b in range(groups):
            stat_s[pl.ds(m * groups + b, 1), :] = rows_to_lanes(
                fold_v[m, pl.ds(b * HD, HD), :]
            )

    wo_in.wait()
    wp_moves = [
        pltpu.make_async_remote_copy(
            wo_v.at[:, pl.ds(pl.multiple_of(col * part, part), part)],
            wp_v.at[j],
            wp_ss.at[j],
            wp_rs.at[j],
            device_id=(me, t1),
            device_id_type=MESH,
        )
        for j, col in enumerate((t1, t3))
    ]
    for copy in wp_moves:
        copy.start()
    w_in[2].wait()

    def v_tile(i, carry):
        k, h = i // 2, lax.rem(i, 2)
        rows = pl.ds(pl.multiple_of(k * span, span), span)
        cols = pl.ds(pl.multiple_of(h * n_half, n_half), n_half)
        v_b[rows, cols] = jnp.dot(
            x_v[rows, :], w_v[2, :, cols], preferred_element_type=jnp.float32
        ).astype(jnp.bfloat16)
        return carry

    lax.fori_loop(0, 4, v_tile, 0)
    stat_moves = [
        pltpu.make_async_remote_copy(
            stat_s,
            stat_r.at[j],
            stat_ss.at[j],
            stat_rs.at[j],
            device_id=peer,
            device_id_type=MESH,
        )
        for j, peer in enumerate(peers)
    ]
    for copy in stat_moves:
        copy.start()
    for copy in moves[1]:
        copy.start()

    lens = [length_ref[order_ref[2 * me + k]] for k in range(2)]
    lane = lax.broadcasted_iota(jnp.int32, (1, HD), 1)
    pair = jnp.where(lane < HALF, lane, lane - HALF).astype(jnp.float32)
    frequency = jnp.exp(pair * (-2.0 / HD * math.log(ROPE_BASE)))
    for k in range(2):

        def angle_tile(b, carry, k=k):
            token = lax.broadcasted_iota(jnp.int32, (HD, 1), 0) + b * HD + lens[k]
            angle = token.astype(jnp.float32) * frequency
            rows = pl.ds(pl.multiple_of(k * span + b * HD, HD), HD)
            cos_v[rows, :] = jnp.cos(angle)
            sine = jnp.sin(angle)
            sin_v[rows, :] = jnp.where(lane < HALF, -sine, sine)
            return carry

        lax.fori_loop(0, span // HD, angle_tile, 0)

    for copy in stat_moves:
        copy.wait_recv()
    square = stat_s[...] + stat_r[0] + stat_r[1] + stat_r[2]
    scale = lax.rsqrt(square / width + NORM_EPS)
    for m in range(2):
        for b in range(groups):
            fold_v[m, pl.ds(b * HD, HD), :] = lanes_to_rows(
                scale[m * groups + b : m * groups + b + 1, :]
            )

    def rope_tile(b, carry):
        rows = pl.ds(pl.multiple_of(b * HD, HD), HD)
        cosine, sine = cos_v[rows, :], sin_v[rows, :]
        for m in range(2):
            by_row = fold_v[m, rows, :]
            for h in range(heads):
                cols = pl.ds(h * HD, HD)
                gain = gain_ref[m : m + 1, h * HD : (h + 1) * HD].astype(jnp.float32)
                value = qk_f[m, rows, cols] * by_row * gain
                turned = value * cosine + pltpu.roll(value, HALF, 1) * sine
                qk_b[m, rows, cols] = turned.astype(jnp.bfloat16)
        return carry

    lax.fori_loop(0, groups, rope_tile, 0)

    for copy in moves[0]:
        copy.wait_recv()
    token_at = lax.broadcasted_iota(jnp.int32, (1, ctx), 1)
    to_base2 = HD**-0.5 * math.log2(math.e)
    causal = lax.broadcasted_iota(jnp.int32, (half, half), 1) <= (
        lax.broadcasted_iota(jnp.int32, (half, half), 0)
    )
    over_rows = (((1,), (1,)), ((), ()))

    def attend(i):
        k, q_at = i // 2, i % 2
        bias = jnp.where(token_at < lens[k], 0.0, NEG)
        seen = half * (q_at + 1)
        new_rows = pl.ds(k * span, seen)

        def head(h, carry):
            cols = pl.ds(pl.multiple_of(h * HD, HD), HD)
            query = qk_b[0, pl.ds(k * span + q_at * half, half), cols]
            old = (
                lax.dot_general(
                    query,
                    cache_v[0, k, :, cols],
                    over_rows,
                    preferred_element_type=jnp.float32,
                )
                + bias
            )
            new = lax.dot_general(
                query,
                qk_b[1, new_rows, cols],
                over_rows,
                preferred_element_type=jnp.float32,
            )
            last = jnp.where(causal, new[:, seen - half :], NEG)
            pieces = [old] + ([new[:, : seen - half]] if q_at else []) + [last]
            top = functools.reduce(
                jnp.maximum, [jnp.max(s, axis=1, keepdims=True) for s in pieces]
            )
            grown = [jnp.exp2((s - top) * to_base2) for s in pieces]
            norm = sum(jnp.sum(e, axis=1, keepdims=True) for e in grown)
            value = jnp.dot(
                grown[0].astype(jnp.bfloat16),
                cache_v[1, k, :, cols],
                preferred_element_type=jnp.float32,
            )
            for j, e in enumerate(grown[1:]):
                value = value + jnp.dot(
                    e.astype(jnp.bfloat16),
                    v_b[pl.ds(k * span + j * half, half), cols],
                    preferred_element_type=jnp.float32,
                )
            att_v[pl.ds(i * half, half), cols] = (value * (1.0 / norm)).astype(
                jnp.bfloat16
            )
            return carry

        lax.fori_loop(0, heads, head, 0)

    att_moves = [
        pltpu.make_async_remote_copy(
            att_v.at[pl.ds(i * half, half)],
            attp_v.at[pl.ds(i * half, half)],
            att_ss.at[i],
            att_rs.at[i],
            device_id=(me, t1),
            device_id_type=MESH,
        )
        for i in range(4)
    ]
    part_moves = [
        pltpu.make_async_remote_copy(
            part_s.at[pl.ds(i * half, half)],
            part_r.at[pl.ds(i * half, half)],
            part_ss.at[i],
            part_rs.at[i],
            device_id=(me, t2),
            device_id_type=MESH,
        )
        for i in range(4)
    ]

    def project(i):
        rows = pl.ds(i * half, half)

        def columns(j, col):
            cols = pl.ds(pl.multiple_of(col * part, part), part)
            return jnp.dot(
                att_v[rows, :], wo_v[:, cols], preferred_element_type=jnp.float32
            ) + jnp.dot(attp_v[rows, :], wp_v[j], preferred_element_type=jnp.float32)

        part_s[rows, :] = columns(1, t2).astype(jnp.bfloat16)
        tot_v[rows, :] = columns(0, t)

    for i in range(4):
        attend(i)
        if i:
            att_moves[i - 1].wait_recv()
            project(i - 1)
            part_moves[i - 1].start()
        att_moves[i].start()
        if i == 0:
            for copy in wp_moves:
                copy.wait_recv()
    att_moves[3].wait_recv()
    project(3)
    part_moves[3].start()
    fin_moves = [
        [
            pltpu.make_async_remote_copy(
                fin_s.at[i],
                fin_r.at[i, j],
                fin_ss.at[i, j],
                fin_rs.at[i, j],
                device_id=peer,
                device_id_type=MESH,
            )
            for j, peer in enumerate(peers)
        ]
        for i in range(4)
    ]
    own_cols = pl.ds(pl.multiple_of(t * part, part), part)

    def finish(i):
        for copy in fin_moves[i]:
            copy.wait_recv()
        square = fin_s[i] + fin_r[i, 0] + fin_r[i, 1] + fin_r[i, 2]
        scale = lax.rsqrt(square / width + NORM_EPS)
        post = post_ref[...].astype(jnp.float32)[None, :]
        for b in range(half // HD):
            rows = pl.ds(i * half + b * HD, HD)
            by_row = lanes_to_rows(scale[b : b + 1, :])
            by_row = jnp.concatenate([by_row] * heads, axis=1)
            normed = tot_v[rows, :] * by_row * post
            res_v[rows, :] = (x_v[rows, own_cols].astype(jnp.float32) + normed).astype(
                jnp.bfloat16
            )

    for i in range(4):
        part_moves[i].wait_recv()
        fin_s[i] = jnp.zeros_like(fin_s[i])
        for b in range(half // HD):
            rows = pl.ds(i * half + b * HD, HD)
            total = tot_v[rows, :] + part_r[rows, :].astype(jnp.float32)
            tot_v[rows, :] = total
            fin_s[i, b : b + 1, :] = rows_to_lanes(lane_fold(total * total))
        for copy in fin_moves[i]:
            copy.start()
        if i:
            finish(i - 1)
    finish(3)

    for copy in moves[1]:
        copy.wait_recv()

    for g in range(2):
        for copy in moves[g]:
            copy.wait_send()
    for copy in wp_moves + stat_moves + att_moves + part_moves:
        copy.wait_send()
    for group in fin_moves:
        for copy in group:
            copy.wait_send()


def store(res_v, cache_v, out_hbm, relaid_hbm, sem):
    copies = [pltpu.make_async_copy(res_v, out_hbm, sem.at[0])] + [
        pltpu.make_async_copy(cache_v.at[plane], relaid_hbm.at[plane], sem.at[1 + plane])
        for plane in range(cache_v.shape[0])
    ]
    for copy in copies:
        copy.start()
    for copy in copies:
        copy.wait()


def on_device(
    span_in, w_qkv, qk_gain, w_out, post_gain, kv_pool, block_table, request_order, lengths
):
    per_device, span, width = span_in.shape
    part = w_qkv.shape[2]
    planes, n_pos, blk, _ = kv_pool.shape
    rows = per_device * span
    n_req = lax.axis_size("req")
    ctx = block_table.shape[1] * blk
    bf16, f32 = jnp.bfloat16, jnp.float32
    vmem, dma = pltpu.VMEM, pltpu.SemaphoreType.DMA
    smem = pl.BlockSpec(memory_space=pltpu.SMEM)
    in_vmem = pl.BlockSpec(memory_space=pltpu.VMEM)
    stay = pl.BlockSpec(memory_space=pl.ANY)
    stat_rows = 2 * rows // HD
    out, relaid = pl.pallas_call(
        kernel,
        name="handover_layer",
        out_shape=(
            vmem((rows, part), bf16),
            vmem((planes, per_device, ctx, part), bf16),
        ),
        in_specs=[smem] * 3 + [in_vmem] * 2 + [stay] * 4,
        out_specs=(in_vmem, in_vmem),
        scratch_shapes=[
            vmem((2, n_pos, blk, part), bf16),
            vmem((2, n_pos, blk, part), bf16),
            vmem((n_req, 2, per_device, blk, part), bf16),
            vmem((n_req, 2, per_device, blk, part), bf16),
            vmem((rows, width), bf16),
            vmem((3, width, part), bf16),
            vmem((part, width), bf16),
            vmem((2, part, part), bf16),
            vmem((2, rows, part), f32),
            vmem((2, rows, part), bf16),
            vmem((rows, part), bf16),
            vmem((2, rows, HD), f32),
            vmem((rows, HD), f32),
            vmem((rows, HD), f32),
            vmem((stat_rows, HD), f32),
            vmem((3, stat_rows, HD), f32),
            vmem((rows, part), bf16),
            vmem((rows, part), bf16),
            vmem((rows, part), bf16),
            vmem((rows, part), bf16),
            vmem((rows, part), f32),
            vmem((4, 8, HD), f32),
            vmem((4, 3, 8, HD), f32),
            dma((8,)),
            dma((2, n_req)),
            dma((2, n_req)),
            dma((2,)),
            dma((2,)),
            dma((3,)),
            dma((3,)),
            dma((4,)),
            dma((4,)),
            dma((4,)),
            dma((4,)),
            dma((4, 3)),
            dma((4, 3)),
        ],
        compiler_params=pltpu.CompilerParams(
            collective_id=0, has_side_effects=True, vmem_limit_bytes=48 << 20
        ),
    )(
        block_table.T,
        request_order,
        lengths,
        qk_gain,
        post_gain,
        span_in.reshape(rows, width),
        w_qkv,
        w_out,
        kv_pool,
    )
    out, relaid = (
        pltpu.with_memory_space_constraint(value, pltpu.VMEM) for value in (out, relaid)
    )
    out, relaid = pl.pallas_call(
        store,
        name="store_outputs",
        out_shape=(
            jax.ShapeDtypeStruct((rows, part), bf16),
            jax.ShapeDtypeStruct((planes, per_device, ctx, part), bf16),
        ),
        in_specs=[in_vmem] * 2,
        out_specs=(stay, stay),
        scratch_shapes=[dma((1 + planes,))],
        compiler_params=pltpu.CompilerParams(vmem_limit_bytes=1 << 20),
    )(out, relaid)
    return out.reshape(per_device, span, part), relaid


def solution(mesh):
    placed = (
        P("req", None, None),
        P(None, None, "tensor"),
        P(None, "tensor"),
        P("tensor", None),
        P("tensor"),
        P(None, "req", None, "tensor"),
        P(),
        P(),
        P(),
    )
    return jax.shard_map(
        on_device,
        mesh=mesh,
        in_specs=placed,
        out_specs=(P("req", None, "tensor"), P(None, "req", None, "tensor")),
        check_vma=False,
    )
```

```python
import functools
import math

import jax
import jax.numpy as jnp
from jax import lax
from jax.experimental import pallas as pl
from jax.experimental.pallas import tpu as pltpu
from jax.sharding import PartitionSpec as P

MESH = pl.DeviceIdType.MESH
HD = 128
HALF = HD // 2
NORM_EPS = 1e-06
ROPE_BASE = 500000.0
GRID = (4, 4, 2)
NEG = -1e30


def far_first():
    steps = [
        (dz, dy, dx)
        for dz in range(GRID[0])
        for dy in range(GRID[1])
        for dx in range(GRID[2])
    ][1:]

    def hops(step):
        dz, dy, dx = step
        return min(dz, GRID[0] - dz) + min(dy, GRID[1] - dy) + 2 * dx

    return sorted(steps, key=lambda step: -hops(step))


def lane_fold(values):
    total = values[:, :HD]
    for low in range(HD, values.shape[1], HD):
        total = total + values[:, low : low + HD]
    return total


def rows_to_lanes(values):
    return jnp.sum(jnp.transpose(values), axis=0, keepdims=True)


def lanes_to_rows(row):
    return jnp.transpose(jnp.broadcast_to(row, (HD, HD)))


def kernel(
    table_ref,
    order_ref,
    length_ref,
    gain_ref,
    post_ref,
    x_hbm,
    wqkv_hbm,
    wout_hbm,
    pool_hbm,
    res_v,
    cache_v,
    pool_a,
    pool_b,
    send_a,
    send_b,
    x_v,
    w_v,
    wo_v,
    wp_v,
    qk_f,
    qk_b,
    v_b,
    fold_v,
    cos_v,
    sin_v,
    stat_s,
    stat_r,
    att_v,
    attp_v,
    part_s,
    part_r,
    tot_v,
    fin_s,
    fin_r,
    load_sem,
    a2a_s,
    a2a_r,
    wp_ss,
    wp_rs,
    stat_ss,
    stat_rs,
    att_ss,
    att_rs,
    part_ss,
    part_rs,
    fin_ss,
    fin_rs,
):
    me = lax.axis_index("req")
    t = lax.axis_index("tensor")
    n_req = lax.axis_size("req")
    chip, core = t // 2, lax.rem(t, 2)
    t1 = chip * 2 + 1 - core
    t2 = (1 - chip) * 2 + core
    t3 = (1 - chip) * 2 + 1 - core
    peers = ((me, t1), (me, t2), (me, t3))
    x_at, y_at, z_at = lax.rem(me, 2), lax.rem(me // 2, 4), me // 8
    steps = far_first()

    def at_step(step):
        dz, dy, dx = step
        return (lax.rem(z_at + dz, 4) * 4 + lax.rem(y_at + dy, 4)) * 2 + lax.rem(
            x_at + dx, 2
        )

    targets = [at_step(step) for step in steps]
    span = x_hbm.shape[0] // 2
    width = x_hbm.shape[1]
    part = v_b.shape[1]
    heads = part // HD
    ctx = cache_v.shape[2]
    blk = pool_hbm.shape[2]
    n_pos = pool_hbm.shape[1]
    half = span // 2

    pool_in = [
        pltpu.make_async_copy(
            pool_hbm.at[pl.ds(2 * g, 2)], (pool_a, pool_b)[g], load_sem.at[g]
        )
        for g in range(2)
    ]
    x_in = [
        pltpu.make_async_copy(
            x_hbm.at[pl.ds(k * span, span)],
            x_v.at[pl.ds(k * span, span)],
            load_sem.at[2 + k],
        )
        for k in range(2)
    ]
    w_in = [
        pltpu.make_async_copy(wqkv_hbm.at[m], w_v.at[m], load_sem.at[4 + m])
        for m in range(3)
    ]
    wo_in = pltpu.make_async_copy(wout_hbm, wo_v, load_sem.at[7])
    barrier = pltpu.get_barrier_semaphore()
    for copy in pool_in:
        copy.start()
    for d in targets:
        pl.semaphore_signal(barrier, inc=1, device_id=(d, t), device_id_type=MESH)
    for peer in peers:
        pl.semaphore_signal(barrier, inc=1, device_id=peer, device_id_type=MESH)
    for copy in (x_in[0], w_in[0], w_in[1], x_in[1], w_in[2], wo_in):
        copy.start()

    sends = (send_a, send_b)

    def gather(g):
        pool_v, send_v = (pool_a, pool_b)[g], sends[g]

        def body(p, carry):
            slot = table_ref[me, order_ref[p]]
            for plane in range(2):
                send_v[p // 2, plane, lax.rem(p, 2)] = pool_v[plane, slot]
            return carry

        lax.fori_loop(0, n_pos, body, 0, unroll=4)
        own = pl.ds(pl.multiple_of(me * blk, blk), blk)
        for plane in range(2):
            for k in range(2):
                cache_v[2 * g + plane, k, own, :] = send_v[me, plane, k]

    def handover(n, g, low, count):
        own = pl.ds(pl.multiple_of(me * blk, blk), blk)
        return [
            pltpu.make_async_remote_copy(
                sends[g].at[d, :, pl.ds(low, count)],
                cache_v.at[pl.ds(2 * g, 2), pl.ds(low, count), own, :],
                a2a_s.at[n, i],
                a2a_r.at[n, i],
                device_id=(d, t),
                device_id_type=MESH,
            )
            for i, d in enumerate(targets)
        ]

    pool_in[0].wait()
    gather(0)
    pl.semaphore_wait(barrier, len(targets) + len(peers))
    moves = [handover(0, 0, 0, 1), handover(1, 0, 1, 1), handover(2, 1, 0, 2)]
    for copy in moves[0] + moves[1]:
        copy.start()
    pool_in[1].wait()
    gather(1)

    x_in[0].wait()
    x_in[1].wait()
    w_in[0].wait()
    w_in[1].wait()
    n_half = part // 2

    def qk_tile(i, carry):
        m, k, h = i // 4, lax.rem(i // 2, 2), lax.rem(i, 2)
        rows = pl.ds(pl.multiple_of(k * span, span), span)
        cols = pl.ds(pl.multiple_of(h * n_half, n_half), n_half)
        tile = jnp.dot(
            x_v[rows, :], w_v[m, :, cols], preferred_element_type=jnp.float32
        )
        qk_f[m, rows, cols] = tile
        fold = lane_fold(tile * tile)

        @pl.when(h == 0)
        def _():
            fold_v[m, rows, :] = fold

        @pl.when(h == 1)
        def _():
            fold_v[m, rows, :] = fold_v[m, rows, :] + fold

        return carry

    lax.fori_loop(0, 8, qk_tile, 0)
    groups = 2 * span // HD
    for m in range(2):
        for b in range(groups):
            stat_s[pl.ds(m * groups + b, 1), :] = rows_to_lanes(
                fold_v[m, pl.ds(b * HD, HD), :]
            )

    wo_in.wait()
    wp_moves = [
        pltpu.make_async_remote_copy(
            wo_v.at[:, pl.ds(pl.multiple_of(col * part, part), part)],
            wp_v.at[j],
            wp_ss.at[j],
            wp_rs.at[j],
            device_id=(me, t1),
            device_id_type=MESH,
        )
        for j, col in enumerate((t1, t3))
    ]
    for copy in wp_moves:
        copy.start()
    w_in[2].wait()

    def v_tile(i, carry):
        k, h = i // 2, lax.rem(i, 2)
        rows = pl.ds(pl.multiple_of(k * span, span), span)
        cols = pl.ds(pl.multiple_of(h * n_half, n_half), n_half)
        v_b[rows, cols] = jnp.dot(
            x_v[rows, :], w_v[2, :, cols], preferred_element_type=jnp.float32
        ).astype(jnp.bfloat16)
        return carry

    lax.fori_loop(0, 4, v_tile, 0)
    stat_moves = [
        pltpu.make_async_remote_copy(
            stat_s,
            stat_r.at[j],
            stat_ss.at[j],
            stat_rs.at[j],
            device_id=peer,
            device_id_type=MESH,
        )
        for j, peer in enumerate(peers)
    ]
    for copy in stat_moves:
        copy.start()
    for copy in moves[2]:
        copy.start()

    lens = [length_ref[order_ref[2 * me + k]] for k in range(2)]
    lane = lax.broadcasted_iota(jnp.int32, (1, HD), 1)
    pair = jnp.where(lane < HALF, lane, lane - HALF).astype(jnp.float32)
    frequency = jnp.exp(pair * (-2.0 / HD * math.log(ROPE_BASE)))
    for k in range(2):

        def angle_tile(b, carry, k=k):
            token = lax.broadcasted_iota(jnp.int32, (HD, 1), 0) + b * HD + lens[k]
            angle = token.astype(jnp.float32) * frequency
            rows = pl.ds(pl.multiple_of(k * span + b * HD, HD), HD)
            cos_v[rows, :] = jnp.cos(angle)
            sine = jnp.sin(angle)
            sin_v[rows, :] = jnp.where(lane < HALF, -sine, sine)
            return carry

        lax.fori_loop(0, span // HD, angle_tile, 0)

    for copy in stat_moves:
        copy.wait_recv()
    square = stat_s[...] + stat_r[0] + stat_r[1] + stat_r[2]
    scale = lax.rsqrt(square / width + NORM_EPS)
    for m in range(2):
        for b in range(groups):
            fold_v[m, pl.ds(b * HD, HD), :] = lanes_to_rows(
                scale[m * groups + b : m * groups + b + 1, :]
            )

    def rope_tile(b, carry):
        rows = pl.ds(pl.multiple_of(b * HD, HD), HD)
        cosine, sine = cos_v[rows, :], sin_v[rows, :]
        for m in range(2):
            by_row = fold_v[m, rows, :]
            for h in range(heads):
                cols = pl.ds(h * HD, HD)
                gain = gain_ref[m : m + 1, h * HD : (h + 1) * HD].astype(jnp.float32)
                value = qk_f[m, rows, cols] * by_row * gain
                turned = value * cosine + pltpu.roll(value, HALF, 1) * sine
                qk_b[m, rows, cols] = turned.astype(jnp.bfloat16)
        return carry

    lax.fori_loop(0, groups, rope_tile, 0)

    for copy in moves[0]:
        copy.wait_recv()
    token_at = lax.broadcasted_iota(jnp.int32, (1, ctx), 1)
    to_base2 = HD**-0.5 * math.log2(math.e)
    causal = lax.broadcasted_iota(jnp.int32, (half, half), 1) <= (
        lax.broadcasted_iota(jnp.int32, (half, half), 0)
    )
    over_rows = (((1,), (1,)), ((), ()))

    def attend(i):
        k, q_at = i // 2, i % 2
        bias = jnp.where(token_at < lens[k], 0.0, NEG)
        seen = half * (q_at + 1)
        new_rows = pl.ds(k * span, seen)

        def head(h, carry):
            cols = pl.ds(pl.multiple_of(h * HD, HD), HD)
            query = qk_b[0, pl.ds(k * span + q_at * half, half), cols]
            old = (
                lax.dot_general(
                    query,
                    cache_v[0, k, :, cols],
                    over_rows,
                    preferred_element_type=jnp.float32,
                )
                + bias
            )
            new = lax.dot_general(
                query,
                qk_b[1, new_rows, cols],
                over_rows,
                preferred_element_type=jnp.float32,
            )
            last = jnp.where(causal, new[:, seen - half :], NEG)
            pieces = [old] + ([new[:, : seen - half]] if q_at else []) + [last]
            top = functools.reduce(
                jnp.maximum, [jnp.max(s, axis=1, keepdims=True) for s in pieces]
            )
            grown = [jnp.exp2((s - top) * to_base2) for s in pieces]
            norm = sum(jnp.sum(e, axis=1, keepdims=True) for e in grown)
            value = jnp.dot(
                grown[0].astype(jnp.bfloat16),
                cache_v[1, k, :, cols],
                preferred_element_type=jnp.float32,
            )
            for j, e in enumerate(grown[1:]):
                value = value + jnp.dot(
                    e.astype(jnp.bfloat16),
                    v_b[pl.ds(k * span + j * half, half), cols],
                    preferred_element_type=jnp.float32,
                )
            att_v[pl.ds(i * half, half), cols] = (value * (1.0 / norm)).astype(
                jnp.bfloat16
            )
            return carry

        lax.fori_loop(0, heads, head, 0)

    att_moves = [
        pltpu.make_async_remote_copy(
            att_v.at[pl.ds(i * half, half)],
            attp_v.at[pl.ds(i * half, half)],
            att_ss.at[i],
            att_rs.at[i],
            device_id=(me, t1),
            device_id_type=MESH,
        )
        for i in range(4)
    ]
    part_moves = [
        pltpu.make_async_remote_copy(
            part_s.at[pl.ds(i * half, half)],
            part_r.at[pl.ds(i * half, half)],
            part_ss.at[i],
            part_rs.at[i],
            device_id=(me, t2),
            device_id_type=MESH,
        )
        for i in range(4)
    ]

    def project(i):
        rows = pl.ds(i * half, half)

        def columns(j, col):
            cols = pl.ds(pl.multiple_of(col * part, part), part)
            return jnp.dot(
                att_v[rows, :], wo_v[:, cols], preferred_element_type=jnp.float32
            ) + jnp.dot(attp_v[rows, :], wp_v[j], preferred_element_type=jnp.float32)

        part_s[rows, :] = columns(1, t2).astype(jnp.bfloat16)
        tot_v[rows, :] = columns(0, t)

    for i in range(4):
        if i == 2:
            for copy in moves[1]:
                copy.wait_recv()
        attend(i)
        if i:
            att_moves[i - 1].wait_recv()
            project(i - 1)
            part_moves[i - 1].start()
        att_moves[i].start()
        if i == 0:
            for copy in wp_moves:
                copy.wait_recv()
    att_moves[3].wait_recv()
    project(3)
    part_moves[3].start()
    fin_moves = [
        [
            pltpu.make_async_remote_copy(
                fin_s.at[i],
                fin_r.at[i, j],
                fin_ss.at[i, j],
                fin_rs.at[i, j],
                device_id=peer,
                device_id_type=MESH,
            )
            for j, peer in enumerate(peers)
        ]
        for i in range(4)
    ]
    own_cols = pl.ds(pl.multiple_of(t * part, part), part)

    def finish(i):
        for copy in fin_moves[i]:
            copy.wait_recv()
        square = fin_s[i] + fin_r[i, 0] + fin_r[i, 1] + fin_r[i, 2]
        scale = lax.rsqrt(square / width + NORM_EPS)
        post = post_ref[...].astype(jnp.float32)[None, :]
        for b in range(half // HD):
            rows = pl.ds(i * half + b * HD, HD)
            by_row = lanes_to_rows(scale[b : b + 1, :])
            by_row = jnp.concatenate([by_row] * heads, axis=1)
            normed = tot_v[rows, :] * by_row * post
            res_v[rows, :] = (x_v[rows, own_cols].astype(jnp.float32) + normed).astype(
                jnp.bfloat16
            )

    for i in range(4):
        part_moves[i].wait_recv()
        fin_s[i] = jnp.zeros_like(fin_s[i])
        for b in range(half // HD):
            rows = pl.ds(i * half + b * HD, HD)
            total = tot_v[rows, :] + part_r[rows, :].astype(jnp.float32)
            tot_v[rows, :] = total
            fin_s[i, b : b + 1, :] = rows_to_lanes(lane_fold(total * total))
        for copy in fin_moves[i]:
            copy.start()
        if i:
            finish(i - 1)
    finish(3)

    for copy in moves[2]:
        copy.wait_recv()

    for group in moves:
        for copy in group:
            copy.wait_send()
    for copy in wp_moves + stat_moves + att_moves + part_moves:
        copy.wait_send()
    for group in fin_moves:
        for copy in group:
            copy.wait_send()


def store(res_v, cache_v, out_hbm, relaid_hbm, sem):
    copies = [pltpu.make_async_copy(res_v, out_hbm, sem.at[0])] + [
        pltpu.make_async_copy(cache_v.at[plane], relaid_hbm.at[plane], sem.at[1 + plane])
        for plane in range(cache_v.shape[0])
    ]
    for copy in copies:
        copy.start()
    for copy in copies:
        copy.wait()


def on_device(
    span_in, w_qkv, qk_gain, w_out, post_gain, kv_pool, block_table, request_order, lengths
):
    per_device, span, width = span_in.shape
    part = w_qkv.shape[2]
    planes, n_pos, blk, _ = kv_pool.shape
    rows = per_device * span
    n_req = lax.axis_size("req")
    ctx = block_table.shape[1] * blk
    bf16, f32 = jnp.bfloat16, jnp.float32
    vmem, dma = pltpu.VMEM, pltpu.SemaphoreType.DMA
    smem = pl.BlockSpec(memory_space=pltpu.SMEM)
    in_vmem = pl.BlockSpec(memory_space=pltpu.VMEM)
    stay = pl.BlockSpec(memory_space=pl.ANY)
    stat_rows = 2 * rows // HD
    out, relaid = pl.pallas_call(
        kernel,
        name="handover_layer",
        out_shape=(
            vmem((rows, part), bf16),
            vmem((planes, per_device, ctx, part), bf16),
        ),
        in_specs=[smem] * 3 + [in_vmem] * 2 + [stay] * 4,
        out_specs=(in_vmem, in_vmem),
        scratch_shapes=[
            vmem((2, n_pos, blk, part), bf16),
            vmem((2, n_pos, blk, part), bf16),
            vmem((n_req, 2, per_device, blk, part), bf16),
            vmem((n_req, 2, per_device, blk, part), bf16),
            vmem((rows, width), bf16),
            vmem((3, width, part), bf16),
            vmem((part, width), bf16),
            vmem((2, part, part), bf16),
            vmem((2, rows, part), f32),
            vmem((2, rows, part), bf16),
            vmem((rows, part), bf16),
            vmem((2, rows, HD), f32),
            vmem((rows, HD), f32),
            vmem((rows, HD), f32),
            vmem((stat_rows, HD), f32),
            vmem((3, stat_rows, HD), f32),
            vmem((rows, part), bf16),
            vmem((rows, part), bf16),
            vmem((rows, part), bf16),
            vmem((rows, part), bf16),
            vmem((rows, part), f32),
            vmem((4, 8, HD), f32),
            vmem((4, 3, 8, HD), f32),
            dma((8,)),
            dma((3, n_req)),
            dma((3, n_req)),
            dma((2,)),
            dma((2,)),
            dma((3,)),
            dma((3,)),
            dma((4,)),
            dma((4,)),
            dma((4,)),
            dma((4,)),
            dma((4, 3)),
            dma((4, 3)),
        ],
        compiler_params=pltpu.CompilerParams(
            collective_id=0, has_side_effects=True, vmem_limit_bytes=48 << 20
        ),
    )(
        block_table.T,
        request_order,
        lengths,
        qk_gain,
        post_gain,
        span_in.reshape(rows, width),
        w_qkv,
        w_out,
        kv_pool,
    )
    out, relaid = (
        pltpu.with_memory_space_constraint(value, pltpu.VMEM) for value in (out, relaid)
    )
    out, relaid = pl.pallas_call(
        store,
        name="store_outputs",
        out_shape=(
            jax.ShapeDtypeStruct((rows, part), bf16),
            jax.ShapeDtypeStruct((planes, per_device, ctx, part), bf16),
        ),
        in_specs=[in_vmem] * 2,
        out_specs=(stay, stay),
        scratch_shapes=[dma((1 + planes,))],
        compiler_params=pltpu.CompilerParams(vmem_limit_bytes=1 << 20),
    )(out, relaid)
    return out.reshape(per_device, span, part), relaid


def solution(mesh):
    placed = (
        P("req", None, None),
        P(None, None, "tensor"),
        P(None, "tensor"),
        P("tensor", None),
        P("tensor"),
        P(None, "req", None, "tensor"),
        P(),
        P(),
        P(),
    )
    return jax.shard_map(
        on_device,
        mesh=mesh,
        in_specs=placed,
        out_specs=(P("req", None, "tensor"), P(None, "req", None, "tensor")),
        check_vma=False,
    )
```
